128 devices in a mesh: day: 16 (over y_lo, x, core), year: 4 (over z), region: 2 (over y_hi).
Axes of the slice: x: 4, y: 4 (y_hi: 2, y_lo: 2; y = y_hi * 2 + y_lo), z: 4, core: 2. Of those that a mesh axis runs over, the one named last changes fastest.
Arguments:
- samples: bfloat16 [368, 8, 2000, 256], P('day', 'year', 'region'), parts along dimension 2, may hold values from -24 to 24, as said below
- counts: int32 [2, 368, 8], P('region', 'day', 'year'), parts along dimension 0, may hold values from 500 to 1000, as said below
Outputs:
- covariance: float32 [2, 368, 256, 256], P('region', 'day', 'year'), parts along dimension 0
- window_mean: float32 [2, 368, 256], P('region', 'day', 'year'), parts along dimension 0
The draws below stay inside these ranges and needn't reach their ends.
There are 2 independent parts, one for each index of `region`. The reference program is written for one: setup_inputs(seed, part) draws one part's arguments, and reference() takes and returns one part's arrays. A program takes and returns all parts, laid end to end along the dimension named above; each array names one. Nothing has to cross between parts.
Inputs may be any that keep to these rules, and one draw needn't show every extreme that they name: `counts`: every entry lies between 500 and 1000; both ends are taken in every draw. `samples`: finite profile values.
All inputs are finite; a program needn't handle non-finite values.
Results may differ from the reference program's by a relative error of at most 0.0003.
Values sent between devices are 32-bit elements; how exact they have to be, the bound alone decides.
A program may use at most 128 MiB of HBM per device.

```python
import math
import jax
import jax.numpy as jnp
from jax import lax

F = 256
HALF = 7
S = 1000
DAYS = 368
GROUPS = 8


def draw_samples(key, part):
    keys = jax.random.split(key, 3)
    shape = (DAYS, GROUPS, S, F)
    feature_scale = 0.3 * jnp.exp(jax.random.uniform(keys[1], (F,), jnp.float32, 0.0, math.log(10.0)))
    day_scale = jnp.exp(jax.random.uniform(keys[2], (DAYS, 1, 1, 1), jnp.float32, -math.log(2.0), math.log(2.0)))
    base = jax.random.truncated_normal(keys[0], -4.0, 4.0, shape, jnp.float32)
    values = base * feature_scale * day_scale
    return values.astype(jnp.bfloat16)


def draw_counts(key, part):
    values = jax.random.randint(key, (1, DAYS, GROUPS), S // 2, S + 1, dtype=jnp.int32)
    values = values.at[0, 0, 0].set(S)
    values = values.at[0, 1, 0].set(S // 2)
    return values


def setup_inputs(seed: int = 0, part: int = 0) -> dict:
    streams_of = jax.random.split(jax.random.key(seed), 3)
    own_keys = jax.random.split(jax.random.fold_in(streams_of[2], part), 3)
    return {
        "samples": draw_samples(jax.random.fold_in(jax.random.fold_in(streams_of[2], part), 71), part),
        "counts": draw_counts(jax.random.fold_in(jax.random.fold_in(streams_of[2], part), 71), part),
    }


def one_day(args):
    day_samples, day_counts = args
    slots = lax.broadcasted_iota(jnp.int32, (day_samples.shape[0], day_samples.shape[1]), 1)
    valid = slots < day_counts[:, None]
    masked = jnp.where(valid[:, :, None], day_samples, jnp.zeros_like(day_samples))
    flat = masked.reshape(-1, masked.shape[-1])
    gram = jnp.dot(flat.T, flat, preferred_element_type=jnp.float32)
    total = jnp.sum(flat, axis=0, dtype=jnp.float32)
    return gram, total


def reference(samples, counts):
    day_gram, day_sum = lax.map(one_day, (samples, counts[0]))
    day_count = jnp.sum(counts[0], axis=1).astype(jnp.float32)
    win_gram = jnp.zeros_like(day_gram)
    win_sum = jnp.zeros_like(day_sum)
    win_count = jnp.zeros_like(day_count)
    for offset in range(-HALF, HALF + 1):
        win_gram = win_gram + jnp.roll(day_gram, -offset, axis=0)
        win_sum = win_sum + jnp.roll(day_sum, -offset, axis=0)
        win_count = win_count + jnp.roll(day_count, -offset, axis=0)
    window_mean = win_sum / win_count[:, None]
    outer = win_count[:, None, None] * window_mean[:, :, None] * window_mean[:, None, :]
    covariance = (win_gram - outer) / (win_count - 1.0)[:, None, None]
    return covariance[None], window_mean[None]
```

```python
import functools

import jax
import jax.numpy as jnp
from jax import lax
from jax.experimental import pallas as pl
from jax.experimental.pallas import tpu as pltpu
from jax.sharding import PartitionSpec as P

HALF = 7
SLOTS = 4
AHEAD = 3
MESH = pl.DeviceIdType.MESH


def kernel(
    low,
    cnt,
    x_ref,
    out_ref,
    win_ref,
    xbuf,
    gram,
    hop,
    ext,
    acc,
    own_s,
    got_s,
    near_s,
    ext_s,
    x_sem,
    o_sem,
    w_sem,
    hop_send,
    hop_recv,
    halo_send,
    halo_recv,
    sum_send,
    sum_recv,
    near_send,
    near_recv,
):
    days, groups, slots, width = x_ref.shape
    z = lax.axis_index("year")
    q = lax.axis_index("day")
    nz = lax.axis_size("year")
    nq = lax.axis_size("day")
    share = width // nz
    after = {"day": lax.rem(q + 1, nq)}
    before = {"day": lax.rem(q + nq - 1, nq)}

    barrier = pltpu.get_barrier_semaphore()
    for j in range(1, nz):
        pl.semaphore_signal(
            barrier, inc=1, device_id={"year": lax.rem(z + j, nz)}, device_id_type=MESH
        )
    pl.semaphore_signal(barrier, inc=1, device_id=after, device_id_type=MESH)
    pl.semaphore_signal(barrier, inc=1, device_id=before, device_id_type=MESH)

    def day_of(i):
        return lax.rem(i + days - HALF, days)

    def step_of(i):
        return 1 + (nz - 2) * lax.rem(i + q, 2)

    def fetch(i):
        slot = lax.rem(i, SLOTS)
        return pltpu.make_async_copy(x_ref.at[day_of(i)], xbuf.at[slot], x_sem.at[slot])

    for i in range(AHEAD):
        fetch(i).start()
    own_s[...] = jnp.zeros_like(own_s)
    pl.semaphore_wait(barrier, nz + 1)

    def block_rows(i, k):
        b = lax.rem(z + (nz - step_of(i)) * (k + 1), nz)
        return pl.ds(pl.multiple_of(b * share, share), share)

    def send(i, k):
        src = gram.at[i, block_rows(i, 0)] if k == 0 else hop.at[k - 1, i]
        return pltpu.make_async_remote_copy(
            src_ref=src,
            dst_ref=hop.at[k, i],
            send_sem=hop_send.at[k, i],
            recv_sem=hop_recv.at[k, i],
            device_id={"year": lax.rem(z + step_of(i), nz)},
            device_id_type=MESH,
        )

    def compute(i):
        slot = lax.rem(i, SLOTS)
        t = day_of(i)
        fetch(i).wait()

        @pl.when(i + AHEAD < days)
        def _():
            fetch(i + AHEAD).start()

        total = jnp.zeros((width, width), jnp.float32)
        sums = jnp.zeros((8, width), jnp.float32)
        count = jnp.int32(0)
        for g in range(groups):
            c = cnt[0, t, g]
            count = count + c
            head = xbuf[slot, g, 0:low, :]
            tail = xbuf[slot, g, low:slots, :]
            rows = low + lax.broadcasted_iota(jnp.int32, tail.shape, 0)
            tail = jnp.where(rows < c, tail, jnp.zeros_like(tail))
            for part in (head, tail):
                total = total + lax.dot_general(
                    part, part, (((0,), (0,)), ((), ())), preferred_element_type=jnp.float32
                )
                ones = jnp.ones((8, part.shape[0]), part.dtype)
                sums = sums + jnp.dot(ones, part, preferred_element_type=jnp.float32)
        gram[i] = total
        mine = lax.broadcasted_iota(jnp.int32, (24, width), 0) == t
        own_s[:, 0:width] = jnp.where(mine, sums[0:1], own_s[:, 0:width])
        counted = jnp.full((24, 128), count, jnp.int32).astype(jnp.float32)
        own_s[:, width:] = jnp.where(mine[:, :128], counted, own_s[:, width:])

    def advance(i, k):
        send(i, k - 1).wait_recv()
        hop[k - 1, i] = hop[k - 1, i] + gram[i, block_rows(i, k)]
        send(i, k).start()

    def first(i, carry):
        compute(i)
        send(i, 0).start()
        return carry

    lax.fori_loop(0, days, first, 0)

    def share_sums(j):
        return pltpu.make_async_remote_copy(
            src_ref=own_s,
            dst_ref=got_s.at[j - 1],
            send_sem=sum_send.at[j - 1],
            recv_sem=sum_recv.at[j - 1],
            device_id={"year": lax.rem(z + j, nz)},
            device_id_type=MESH,
        )

    for j in range(1, nz):
        share_sums(j).start()

    def second(i, carry):
        advance(i, 1)
        return carry

    lax.fori_loop(0, days, second, 0)

    for j in range(1, nz):
        share_sums(j).wait()
    merged = own_s[...]
    for j in range(1, nz):
        merged = merged + got_s[j - 1]
    last = days - HALF
    ext_s[...] = jnp.zeros_like(ext_s)
    ext_s[HALF : HALF + days] = merged[0:days]
    own_s[...] = merged

    def near(side):
        rows = pl.ds(last if side == 0 else 0, 8)
        return pltpu.make_async_remote_copy(
            src_ref=own_s.at[rows],
            dst_ref=near_s.at[side],
            send_sem=near_send.at[side],
            recv_sem=near_recv.at[side],
            device_id=after if side == 0 else before,
            device_id_type=MESH,
        )

    def third(i, carry):
        advance(i, 2)
        return carry

    lax.fori_loop(0, days, third, 0)
    for side in range(2):
        near(side).start()

    def halo(i, to_after):
        t = day_of(i)
        return pltpu.make_async_remote_copy(
            src_ref=ext.at[t + HALF],
            dst_ref=ext.at[t - last if to_after else t + HALF + days],
            send_sem=halo_send.at[i],
            recv_sem=halo_recv.at[i],
            device_id=after if to_after else before,
            device_id_type=MESH,
        )

    def finish(i):
        send(i, 2).wait_recv()
        ext[day_of(i) + HALF] = hop[2, i] + gram[i, block_rows(i, 3)]

    def edge_after(i, carry):
        finish(i)
        halo(i, True).start()
        return carry

    def edge_before(i, carry):
        finish(i)
        halo(i, False).start()
        return carry

    def inner(i, carry):
        finish(i)
        return carry

    lax.fori_loop(0, HALF, edge_after, 0)
    lax.fori_loop(HALF, 2 * HALF, edge_before, 0)
    lax.fori_loop(2 * HALF, days, inner, 0)

    for side in range(2):
        near(side).wait()
    ext_s[0:HALF] = near_s[0, 0:HALF]
    ext_s[HALF + days : 2 * HALF + days] = near_s[1, 0:HALF]
    win = ext_s[0:24]
    for k in range(1, 2 * HALF + 1):
        win = win + ext_s[k : k + 24]
    own_s[...] = win
    win_copy = pltpu.make_async_copy(own_s, win_ref, w_sem)
    win_copy.start()

    def wait_after(i, carry):
        halo(i, True).wait()
        return carry

    def wait_before(i, carry):
        halo(i, False).wait()
        return carry

    lax.fori_loop(0, HALF, wait_after, 0)
    lax.fori_loop(HALF, 2 * HALF, wait_before, 0)

    def window(d, carry):
        total = ext[d]
        for k in range(1, 2 * HALF + 1):
            total = total + ext[d + k]
        acc[d] = total
        return carry

    lax.fori_loop(0, days, window, 0)
    whole = pltpu.make_async_copy(acc, out_ref, o_sem)
    whole.start()

    def drain(i, carry):
        for k in range(nz - 1):
            send(i, k).wait_send()
        return carry

    lax.fori_loop(0, days, drain, 0)
    win_copy.wait()
    whole.wait()


def shards(samples, counts):
    days, groups, slots, width = samples.shape
    nz = lax.axis_size("year")
    share = width // nz
    low = slots // 2 // 16 * 16
    f32 = jnp.float32
    dma = pltpu.SemaphoreType.DMA
    gram, win = pl.pallas_call(
        functools.partial(kernel, low),
        out_shape=(
            jax.ShapeDtypeStruct((days, share, width), f32),
            jax.ShapeDtypeStruct((24, width + 128), f32),
        ),
        in_specs=[
            pl.BlockSpec(memory_space=pltpu.SMEM),
            pl.BlockSpec(memory_space=pl.ANY),
        ],
        out_specs=(pl.BlockSpec(memory_space=pl.ANY), pl.BlockSpec(memory_space=pl.ANY)),
        scratch_shapes=[
            pltpu.VMEM((SLOTS, groups, slots, width), samples.dtype),
            pltpu.VMEM((days, width, width), f32),
            pltpu.VMEM((nz - 1, days, share, width), f32),
            pltpu.VMEM((days + 2 * HALF, share, width), f32),
            pltpu.VMEM((days, share, width), f32),
            pltpu.VMEM((24, width + 128), f32),
            pltpu.VMEM((nz - 1, 24, width + 128), f32),
            pltpu.VMEM((2, 8, width + 128), f32),
            pltpu.VMEM((40, width + 128), f32),
            dma((SLOTS,)),
            dma,
            dma,
            dma((nz - 1, days)),
            dma((nz - 1, days)),
            dma((2 * HALF,)),
            dma((2 * HALF,)),
            dma((nz - 1,)),
            dma((nz - 1,)),
            dma((2,)),
            dma((2,)),
        ],
        compiler_params=pltpu.CompilerParams(
            collective_id=0, has_side_effects=True, vmem_limit_bytes=56 * 2**20
        ),
    )(counts, samples)
    win_sum = win[:days, :width]
    win_count = win[:days, width]
    full_mean = win_sum / win_count[:, None]
    start = lax.axis_index("year") * share
    own_mean = lax.dynamic_slice_in_dim(full_mean, start, share, 1)
    outer = win_count[:, None, None] * own_mean[:, :, None] * full_mean[:, None, :]
    covariance = (gram - outer) / (win_count - 1.0)[:, None, None]
    return (covariance[None], own_mean[None])


def solution(mesh):
    placed = (P("day", "year", "region", None), P("region", "day", "year"))
    return jax.shard_map(
        shards,
        mesh=mesh,
        in_specs=placed,
        out_specs=(P("region", "day", "year", None), P("region", "day", "year")),
        check_vma=False,
    )
```

```python
import functools

import jax
import jax.numpy as jnp
from jax import lax
from jax.experimental import pallas as pl
from jax.experimental.pallas import tpu as pltpu
from jax.sharding import PartitionSpec as P

HALF = 7
SPAN = 2 * HALF + 1
SLOTS = 4
AHEAD = 3
LANES = 128
LAG1 = 4
LAG3 = 3
LAG4 = 6
LAG5 = 11
MESH = pl.DeviceIdType.MESH


def turned(x):
    return pltpu.roll(x, LANES // 2, 1)


def flipped(x):
    return jnp.concatenate([x, x], axis=0).T


def kernel(
    low,
    cnt_ref,
    x_ref,
    out_ref,
    mean_ref,
    cnt,
    xbuf,
    pack,
    hop,
    give,
    take,
    tile,
    ext,
    acc,
    own_s,
    got_s,
    mrg_s,
    near_s,
    ext_s,
    mean_s,
    inv_s,
    own_m,
    c_sem,
    x_sem,
    o_sem,
    m_sem,
    hop_send,
    hop_recv,
    give_send,
    give_recv,
    halo_send,
    halo_recv,
    sum_send,
    sum_recv,
    near_send,
    near_recv,
):
    days, groups, slots, width = x_ref.shape
    f32 = jnp.float32
    z = lax.axis_index("year")
    q = lax.axis_index("day")
    nz = lax.axis_size("year")
    nq = lax.axis_size("day")
    share = width // nz
    quarter = share // nz
    rows = share + quarter
    low32 = share // 2
    last = days - HALF
    even = lax.rem(z, 2) == 0
    after = {"day": lax.rem(q + 1, nq)}
    before = {"day": lax.rem(q + nq - 1, nq)}

    def peer(j):
        return {"year": lax.rem(z + j, nz)}

    def left(n):
        return lax.broadcasted_iota(jnp.int32, (n, LANES), 1) < LANES // 2

    barrier = pltpu.get_barrier_semaphore()
    for j in range(1, nz):
        pl.semaphore_signal(barrier, inc=1, device_id=peer(j), device_id_type=MESH)
    pl.semaphore_signal(barrier, inc=1, device_id=after, device_id_type=MESH)
    pl.semaphore_signal(barrier, inc=1, device_id=before, device_id_type=MESH)

    def day_of(i):
        return lax.rem(i + last, days)

    def step_of(i):
        return 1 + (nz - 2) * lax.rem(i + q, 2)

    def fetch(i):
        slot = lax.rem(i, SLOTS)
        return pltpu.make_async_copy(x_ref.at[day_of(i)], xbuf.at[slot], x_sem.at[slot])

    counted = pltpu.make_async_copy(cnt_ref, cnt, c_sem)
    counted.start()
    for i in range(AHEAD):
        fetch(i).start()
    own_s[...] = jnp.zeros_like(own_s)
    ext_s[...] = jnp.zeros_like(ext_s)

    def clear(e, carry):
        acc[e] = jnp.zeros((share, width), f32)
        return carry

    lax.fori_loop(0, days + 4 * HALF, clear, 0)
    counted.wait()

    def compute(i):
        slot = lax.rem(i, SLOTS)
        t = day_of(i)
        fetch(i).wait()

        @pl.when(i + AHEAD < days)
        def _():
            fetch(i + AHEAD).start()

        total = jnp.zeros((width, width), f32)
        sums = jnp.zeros((8, width), f32)
        count = jnp.int32(0)
        for g in range(groups):
            c = cnt[g, t]
            count = count + c
            head = xbuf[slot, g, 0:low, :]
            tail = xbuf[slot, g, low:slots, :]
            at = low + lax.broadcasted_iota(jnp.int32, tail.shape, 0)
            tail = jnp.where(at < c, tail, jnp.zeros_like(tail))
            for part in (head, tail):
                total = total + lax.dot_general(
                    part, part, (((0,), (0,)), ((), ())), preferred_element_type=f32
                )
                ones = jnp.ones((8, part.shape[0]), part.dtype)
                sums = sums + jnp.dot(ones, part, preferred_element_type=f32)
        half = left(share)

        def cell(r, h):
            return total[share * r : share * (r + 1), LANES * h : LANES * (h + 1)]

        main = (
            cell(0, 0),
            jnp.where(half, cell(1, 1), cell(1, 0)),
            cell(2, 1),
            jnp.where(half, cell(3, 0), cell(3, 1)),
        )
        across = jnp.where(half, cell(0, 1), cell(1, 1))
        for b in range(4):
            pack[i, b, 0:share] = main[b]
            pack[i, b, share:rows] = across[quarter * b : quarter * (b + 1)]
        line = lax.broadcasted_iota(jnp.int32, (24, width), 0)
        lane = lax.broadcasted_iota(jnp.int32, (24, width), 1)
        kept = jnp.where(line == t, sums[0:1], own_s[...])
        number = jnp.full((24, width), count, jnp.int32).astype(f32)
        own_s[...] = jnp.where((line == days) & (lane == t), number, kept)

    def block(i, k):
        return lax.rem(z + (nz - step_of(i)) * (k + 1), nz)

    def send(i, k):
        return pltpu.make_async_remote_copy(
            src_ref=pack.at[i, block(i, 0)] if k == 0 else hop.at[k - 1, i],
            dst_ref=hop.at[k, i],
            send_sem=hop_send.at[k, i],
            recv_sem=hop_recv.at[k, i],
            device_id=peer(step_of(i)),
            device_id_type=MESH,
        )

    def advance(i, k):
        send(i, k - 1).wait_recv()
        hop[k - 1, i] = hop[k - 1, i] + pack[i, block(i, k)]
        send(i, k).start()

    def give_to(i, j):
        start, size, land = ((0, 40, 0), (40, 8, 48), (32, 8, 40))[j - 1]
        return pltpu.make_async_remote_copy(
            src_ref=give.at[i, pl.ds(start, size)],
            dst_ref=take.at[i, pl.ds(land, size)],
            send_sem=give_send.at[j - 1, i],
            recv_sem=give_recv.at[j - 1, i],
            device_id=peer(j),
            device_id_type=MESH,
        )

    def reduce_last(i):
        send(i, 2).wait_recv()
        mine = hop[2, i] + pack[i, z]
        hop[2, i] = mine
        both = flipped(mine[0:share])
        turn = jnp.where(even, both[share:], both[:share])
        edge = mine[share:rows]
        edge_t = turned(edge)
        half8 = left(8)
        lefts = jnp.where(half8, edge[0:8], edge_t[8:16])
        rights = jnp.where(half8, edge_t[0:8], edge[8:16])
        give[i, 0:low32] = jnp.where(left(low32), turn[0:low32], turn[low32:])
        give[i, 32:40] = jnp.where(even, rights, lefts)
        give[i, 40:48] = jnp.where(even, lefts, rights)
        for j in range(1, nz):
            give_to(i, j).start()

    def halo(i):
        side = i // HALF
        return pltpu.make_async_remote_copy(
            src_ref=ext.at[day_of(i) + HALF],
            dst_ref=ext.at[i + days * side],
            send_sem=halo_send.at[i],
            recv_sem=halo_recv.at[i],
            device_id={"day": lax.rem(q + 1 + (nq - 2) * side, nq)},
            device_id_type=MESH,
        )

    def add_day(e):
        value = ext[e]

        def one(k, carry):
            acc[e + k] = acc[e + k] + value
            return carry

        lax.fori_loop(0, SPAN, one, 0)

    def assemble(i):
        for j in range(1, nz):
            give_to(i, j).wait_recv()
        pieces = (give[i, 40:48], take[i, 40:48], take[i, 48:56], take[i, 32:40])
        for j, piece in enumerate(pieces):
            at = quarter * lax.rem(z + j, nz)
            tile[pl.ds(pl.multiple_of(at, 8), 8)] = piece
            tile[pl.ds(pl.multiple_of(at + 8, 8), 8)] = turned(piece)
        flat = tile[...]
        straight = jnp.where(z == 0, flat, turned(flat))
        opposite = jnp.where(z < 2, straight, flipped(flat)[:share])
        near_p = take[i, 0:32]
        near_t = turned(near_p)
        beside = jnp.where(
            even,
            jnp.concatenate([near_t, near_p], axis=0),
            jnp.concatenate([near_p, near_t], axis=0),
        )
        lane = lax.broadcasted_iota(jnp.int32, (share, LANES), 1) // (LANES // 2)
        other = jnp.where(lane == lax.rem(z, 2), opposite, beside)
        left_main = 1 - lax.rem((z + 1) // 2, 2)
        right_main = 1 - z // 2
        use = jnp.where(lane == 0, left_main, right_main) == 1
        main = hop[2, i, 0:share]
        e = day_of(i) + HALF
        ext[e, :, 0:LANES] = jnp.where(use, main, other)
        ext[e, :, LANES:] = jnp.where(use, other, main)

        @pl.when(i < 2 * HALF)
        def _():
            halo(i).start()

        add_day(e)

    def add_halo(i):
        halo(i).wait_recv()
        add_day(i + days * (i // HALF))

    def put(d):
        return pltpu.make_async_copy(acc.at[d + 2 * HALF], out_ref.at[d], o_sem.at[d])

    def close(d):
        scale = inv_s[d][0:1]
        acc[d + 2 * HALF, :, 0:LANES] = acc[d + 2 * HALF, :, 0:LANES] * scale
        acc[d + 2 * HALF, :, LANES:] = acc[d + 2 * HALF, :, LANES:] * scale
        put(d).start()

    compute(0)
    pl.semaphore_wait(barrier, nz + 1)
    send(0, 0).start()

    def first(v, carry):
        compute(v)
        send(v, 0).start()

        @pl.when(v >= LAG1)
        def _():
            advance(v - LAG1, 1)

        return carry

    lax.fori_loop(1, days, first, 0)

    def share_sums(j):
        return pltpu.make_async_remote_copy(
            src_ref=own_s,
            dst_ref=got_s.at[j - 1],
            send_sem=sum_send.at[j - 1],
            recv_sem=sum_recv.at[j - 1],
            device_id=peer(j),
            device_id_type=MESH,
        )

    for j in range(1, nz):
        share_sums(j).start()

    stages = (
        (LAG1 - days, days - LAG1, days, lambda i: advance(i, 1)),
        (0, 0, days, lambda i: advance(i, 2)),
        (LAG3, 0, days, reduce_last),
        (LAG4, 0, days, assemble),
        (LAG5, 0, 2 * HALF, add_halo),
        (LAG4 + 2 * HALF, 0, HALF + 1, close),
    )

    def run(begin, end):
        def body(v, carry):
            for lag, lo, hi, stage in stages:
                i = v - lag
                if end - lag <= lo or begin - lag >= hi:
                    continue
                if begin - lag >= lo and end - lag <= hi:
                    stage(i)
                else:
                    pl.when((i >= lo) & (i < hi))(functools.partial(stage, i))
            return carry

        lax.fori_loop(begin, end, body, 0)

    def near(side):
        at = pl.ds(last if side == 0 else 0, 8)
        return pltpu.make_async_remote_copy(
            src_ref=mrg_s.at[at],
            dst_ref=near_s.at[side],
            send_sem=near_send.at[side],
            recv_sem=near_recv.at[side],
            device_id=after if side == 0 else before,
            device_id_type=MESH,
        )

    run(0, 5)
    for j in range(1, nz):
        share_sums(j).wait()
    merged = own_s[...]
    for j in range(1, nz):
        merged = merged + got_s[j - 1]
    line = lax.broadcasted_iota(jnp.int32, (24, LANES), 0)
    lane = lax.broadcasted_iota(jnp.int32, (24, LANES), 1)
    number = jnp.where(line == lane, merged[days : days + 1, 0:LANES], 0.0)
    number = jnp.sum(number, axis=1, keepdims=True)
    mrg_s[:, 0:width] = merged
    mrg_s[:, width:] = jnp.broadcast_to(number, (24, LANES))
    for side in range(2):
        near(side).start()
    ext_s[HALF : HALF + days] = mrg_s[0:days]

    run(5, 10)
    for side in range(2):
        near(side).wait()
    ext_s[0:HALF] = near_s[0, 0:HALF]
    ext_s[HALF + days : 2 * HALF + days] = near_s[1, 0:HALF]
    win = ext_s[0:24]
    for k in range(1, SPAN):
        win = win + ext_s[k : k + 24]
    win_sum = win[:, 0:width]
    win_count = win[:, width:]
    mean_s[:, 0:LANES] = win_sum[:, 0:LANES] / win_count
    mean_s[:, LANES:] = win_sum[:, LANES:] / win_count
    inverse = 1.0 / (win_count - 1.0)
    own = mean_s[:, pl.ds(pl.multiple_of(LANES * (z // 2), LANES), LANES)]
    own = jnp.where(even, own, turned(own))
    own_m[...] = own
    mean_copy = pltpu.make_async_copy(own_m, mean_ref, m_sem)
    mean_copy.start()
    column = jnp.concatenate([own, jnp.zeros((LANES - 24, LANES), f32)], axis=0).T[:share]
    for d in range(days):
        inv_s[d] = jnp.broadcast_to(inverse[d : d + 1], (8, LANES))
        outer = column[:, d : d + 1] * win_sum[d : d + 1]
        acc[d + 2 * HALF] = acc[d + 2 * HALF] - outer

    run(10, days + LAG4)

    def rest(d, carry):
        close(d)
        return carry

    lax.fori_loop(HALF + 1, days, rest, 0)

    def drain(i, carry):
        for k in range(nz - 1):
            send(i, k).wait_send()
            give_to(i, k + 1).wait_send()
        return carry

    lax.fori_loop(0, days, drain, 0)

    def drain_halo(i, carry):
        halo(i).wait_send()
        return carry

    lax.fori_loop(0, 2 * HALF, drain_halo, 0)
    mean_copy.wait()

    def written(d, carry):
        put(d).wait()
        return carry

    lax.fori_loop(0, days, written, 0)


def shards(samples, counts):
    days, groups, slots, width = samples.shape
    nz = lax.axis_size("year")
    share = width // nz
    rows = share + share // nz
    low = slots // 2 // 16 * 16
    f32 = jnp.float32
    dma = pltpu.SemaphoreType.DMA
    covariance, mean = pl.pallas_call(
        functools.partial(kernel, low),
        out_shape=(
            jax.ShapeDtypeStruct((days, share, width), f32),
            jax.ShapeDtypeStruct((24, LANES), f32),
        ),
        in_specs=[pl.BlockSpec(memory_space=pl.ANY), pl.BlockSpec(memory_space=pl.ANY)],
        out_specs=(pl.BlockSpec(memory_space=pl.ANY), pl.BlockSpec(memory_space=pl.ANY)),
        scratch_shapes=[
            pltpu.SMEM((groups, days), jnp.int32),
            pltpu.VMEM((SLOTS, groups, slots, width), samples.dtype),
            pltpu.VMEM((days, nz, rows, LANES), f32),
            pltpu.VMEM((nz - 1, days, rows, LANES), f32),
            pltpu.VMEM((days, 48, LANES), f32),
            pltpu.VMEM((days, 56, LANES), f32),
            pltpu.VMEM((share, LANES), f32),
            pltpu.VMEM((days + 2 * HALF, share, width), f32),
            pltpu.VMEM((days + 4 * HALF, share, width), f32),
            pltpu.VMEM((24, width), f32),
            pltpu.VMEM((nz - 1, 24, width), f32),
            pltpu.VMEM((24, width + LANES), f32),
            pltpu.VMEM((2, 8, width + LANES), f32),
            pltpu.VMEM((40, width + LANES), f32),
            pltpu.VMEM((24, width), f32),
            pltpu.VMEM((days, 8, LANES), f32),
            pltpu.VMEM((24, LANES), f32),
            dma,
            dma((SLOTS,)),
            dma((days,)),
            dma,
            dma((nz - 1, days)),
            dma((nz - 1, days)),
            dma((nz - 1, days)),
            dma((nz - 1, days)),
            dma((2 * HALF,)),
            dma((2 * HALF,)),
            dma((nz - 1,)),
            dma((nz - 1,)),
            dma((2,)),
            dma((2,)),
        ],
        compiler_params=pltpu.CompilerParams(
            collective_id=0, has_side_effects=True, vmem_limit_bytes=56 * 2**20
        ),
    )(jnp.swapaxes(counts, 1, 2)[0], samples)
    return (covariance[None], mean[:days, :share][None])


def solution(mesh):
    placed = (P("day", "year", "region", None), P("region", "day", "year"))
    return jax.shard_map(
        shards,
        mesh=mesh,
        in_specs=placed,
        out_specs=(P("region", "day", "year", None), P("region", "day", "year")),
        check_vma=False,
    )
```

```python
import functools

import jax
import jax.numpy as jnp
from jax import lax
from jax.experimental import pallas as pl
from jax.experimental.pallas import tpu as pltpu
from jax.sharding import PartitionSpec as P

HALF = 7
SPAN = 2 * HALF + 1
SLOTS = 8
AHEAD = 7
LANES = 128
LAG1 = 8
LAG3 = 6
LAG4 = 12
LAG5 = 17
MESH = pl.DeviceIdType.MESH


def turned(x):
    return pltpu.roll(x, LANES // 2, 1)


def flipped(x):
    return jnp.concatenate([x, x], axis=0).T


def kernel(
    low,
    cnt_ref,
    x_ref,
    out_ref,
    mean_ref,
    cnt,
    xbuf,
    pack,
    hop,
    give,
    take,
    tile,
    ext,
    acc,
    own_s,
    got_s,
    mrg_s,
    near_s,
    ext_s,
    mean_s,
    inv_s,
    own_m,
    c_sem,
    x_sem,
    o_sem,
    m_sem,
    hop_send,
    hop_recv,
    give_send,
    give_recv,
    halo_send,
    halo_recv,
    sum_send,
    sum_recv,
    near_send,
    near_recv,
):
    days, groups, slots, width = x_ref.shape
    f32 = jnp.float32
    z = lax.axis_index("year")
    q = lax.axis_index("day")
    nz = lax.axis_size("year")
    nq = lax.axis_size("day")
    share = width // nz
    quarter = share // nz
    rows = share + quarter
    low32 = share // 2
    last = days - HALF
    even = lax.rem(z, 2) == 0
    after = {"day": lax.rem(q + 1, nq)}
    before = {"day": lax.rem(q + nq - 1, nq)}

    def peer(j):
        return {"year": lax.rem(z + j, nz)}

    def left(n):
        return lax.broadcasted_iota(jnp.int32, (n, LANES), 1) < LANES // 2

    barrier = pltpu.get_barrier_semaphore()
    for j in range(1, nz):
        pl.semaphore_signal(barrier, inc=1, device_id=peer(j), device_id_type=MESH)
    pl.semaphore_signal(barrier, inc=1, device_id=after, device_id_type=MESH)
    pl.semaphore_signal(barrier, inc=1, device_id=before, device_id_type=MESH)

    def day_of(i):
        return lax.rem(i + last, days)

    def step_of(i):
        return 1 + (nz - 2) * lax.rem(i + q, 2)

    def fetch(i):
        slot = lax.rem(i, SLOTS)
        return pltpu.make_async_copy(x_ref.at[day_of(i)], xbuf.at[slot], x_sem.at[slot])

    counted = pltpu.make_async_copy(cnt_ref, cnt, c_sem)
    counted.start()
    for i in range(AHEAD):
        fetch(i).start()
    own_s[...] = jnp.zeros_like(own_s)
    ext_s[...] = jnp.zeros_like(ext_s)

    def clear(e, carry):
        acc[e] = jnp.zeros((share, width), f32)
        return carry

    lax.fori_loop(0, days + 4 * HALF, clear, 0)
    counted.wait()

    def compute(i):
        slot = lax.rem(i, SLOTS)
        t = day_of(i)
        fetch(i).wait()

        @pl.when(i + AHEAD < days)
        def _():
            fetch(i + AHEAD).start()

        total = jnp.zeros((width, width), f32)
        sums = jnp.zeros((8, width), f32)
        count = jnp.int32(0)
        for g in range(groups):
            c = cnt[g, t]
            count = count + c
            head = xbuf[slot, g, 0:low, :]
            tail = xbuf[slot, g, low:slots, :]
            at = low + lax.broadcasted_iota(jnp.int32, tail.shape, 0)
            tail = jnp.where(at < c, tail, jnp.zeros_like(tail))
            for part in (head, tail):
                total = total + lax.dot_general(
                    part, part, (((0,), (0,)), ((), ())), preferred_element_type=f32
                )
                sums = sums + jnp.sum(part.astype(f32).reshape(-1, 8, width), axis=0)
        half = left(share)

        def cell(r, h):
            return total[share * r : share * (r + 1), LANES * h : LANES * (h + 1)]

        lane_no = lax.broadcasted_iota(jnp.int32, (share, LANES), 1)
        wide = lane_no * 0 + step_of(i) == 1
        main = (
            jnp.where(half | wide, cell(0, 0), cell(0, 1)),
            jnp.where(half & wide, cell(1, 1), cell(1, 0)),
            jnp.where(half | wide, cell(2, 1), cell(2, 0)),
            jnp.where(half & wide, cell(3, 0), cell(3, 1)),
        )
        across = jnp.where(half, cell(0, 1), cell(1, 1))
        for b in range(4):
            pack[i, b, 0:share] = main[b]
            pack[i, b, share:rows] = across[quarter * b : quarter * (b + 1)]
        line = lax.broadcasted_iota(jnp.int32, (24, width), 0)
        lane = lax.broadcasted_iota(jnp.int32, (24, width), 1)
        kept = jnp.where(line == t, jnp.sum(sums, axis=0, keepdims=True), own_s[...])
        number = jnp.full((24, width), count, jnp.int32).astype(f32)
        own_s[...] = jnp.where((line == days) & (lane == t), number, kept)

    def block(i, k):
        return lax.rem(z + (nz - step_of(i)) * (k + 1), nz)

    def send(i, k):
        return pltpu.make_async_remote_copy(
            src_ref=pack.at[i, block(i, 0)] if k == 0 else hop.at[k - 1, i],
            dst_ref=hop.at[k, i],
            send_sem=hop_send.at[k, i],
            recv_sem=hop_recv.at[k, i],
            device_id=peer(step_of(i)),
            device_id_type=MESH,
        )

    def advance(i, k):
        send(i, k - 1).wait_recv()
        hop[k - 1, i] = hop[k - 1, i] + pack[i, block(i, k)]
        send(i, k).start()

    def give_to(i, j):
        start, size, land = ((0, 40, 0), (40, 8, 48), (32, 8, 40))[j - 1]
        to = (step_of(i), 2, nz - step_of(i))[j - 1]
        return pltpu.make_async_remote_copy(
            src_ref=give.at[i, pl.ds(start, size)],
            dst_ref=take.at[i, pl.ds(land, size)],
            send_sem=give_send.at[j - 1, i],
            recv_sem=give_recv.at[j - 1, i],
            device_id=peer(to),
            device_id_type=MESH,
        )

    def reduce_last(i):
        send(i, 2).wait_recv()
        mine = hop[2, i] + pack[i, z]
        hop[2, i] = mine
        both = flipped(mine[0:share])
        turn = jnp.where(even, both[share:], both[:share])
        edge = mine[share:rows]
        edge_t = turned(edge)
        half8 = left(8)
        lefts = jnp.where(half8, edge[0:8], edge_t[8:16])
        rights = jnp.where(half8, edge_t[0:8], edge[8:16])
        give[i, 0:low32] = jnp.where(left(low32), turn[0:low32], turn[low32:])
        give[i, 32:40] = jnp.where(even, rights, lefts)
        give[i, 40:48] = jnp.where(even, lefts, rights)
        for j in range(1, nz):
            give_to(i, j).start()

    def halo(i):
        side = i // HALF
        return pltpu.make_async_remote_copy(
            src_ref=ext.at[day_of(i) + HALF],
            dst_ref=ext.at[i + days * side],
            send_sem=halo_send.at[i],
            recv_sem=halo_recv.at[i],
            device_id={"day": lax.rem(q + 1 + (nq - 2) * side, nq)},
            device_id_type=MESH,
        )

    def add_day(e):
        value = ext[e]

        def one(k, carry):
            acc[e + k] = acc[e + k] + value
            return carry

        lax.fori_loop(0, SPAN, one, 0)

    def assemble(i):
        for j in range(1, nz):
            give_to(i, j).wait_recv()
        pieces = (give[i, 40:48], take[i, 40:48], take[i, 48:56], take[i, 32:40])
        s = step_of(i)
        for j, piece in zip((0, s, 2, nz - s), pieces):
            at = quarter * lax.rem(z + j, nz)
            tile[pl.ds(pl.multiple_of(at, 8), 8)] = piece
            tile[pl.ds(pl.multiple_of(at + 8, 8), 8)] = turned(piece)
        flat = tile[...]
        straight = jnp.where(z == 0, flat, turned(flat))
        opposite = jnp.where(z < 2, straight, flipped(flat)[:share])
        near_p = take[i, 0:32]
        near_t = turned(near_p)
        beside = jnp.where(
            even,
            jnp.concatenate([near_t, near_p], axis=0),
            jnp.concatenate([near_p, near_t], axis=0),
        )
        lane = lax.broadcasted_iota(jnp.int32, (share, LANES), 1) // (LANES // 2)
        other = jnp.where(lane == lax.rem(z, 2), opposite, beside)
        own_main = 1 - z // 2
        next_main = 1 - lax.rem(z + s, nz) // 2
        use = jnp.where(lane == lax.rem(z, 2), own_main, next_main) == 1
        main = hop[2, i, 0:share]
        e = day_of(i) + HALF
        ext[e, :, 0:LANES] = jnp.where(use, main, other)
        ext[e, :, LANES:] = jnp.where(use, other, main)

        @pl.when(i < 2 * HALF)
        def _():
            halo(i).start()

        add_day(e)

    def add_halo(i):
        halo(i).wait_recv()
        add_day(i + days * (i // HALF))

    def put(d):
        return pltpu.make_async_copy(acc.at[d + 2 * HALF], out_ref.at[d], o_sem.at[d])

    def close(d):
        scale = inv_s[d][0:1]
        acc[d + 2 * HALF, :, 0:LANES] = acc[d + 2 * HALF, :, 0:LANES] * scale
        acc[d + 2 * HALF, :, LANES:] = acc[d + 2 * HALF, :, LANES:] * scale
        put(d).start()

    compute(0)
    pl.semaphore_wait(barrier, nz + 1)
    send(0, 0).start()

    def first(v, carry):
        compute(v)
        send(v, 0).start()

        @pl.when(v >= LAG1)
        def _():
            advance(v - LAG1, 1)

        return carry

    lax.fori_loop(1, days, first, 0)

    def share_sums(j):
        return pltpu.make_async_remote_copy(
            src_ref=own_s,
            dst_ref=got_s.at[j - 1],
            send_sem=sum_send.at[j - 1],
            recv_sem=sum_recv.at[j - 1],
            device_id=peer(j),
            device_id_type=MESH,
        )

    for j in range(1, nz):
        share_sums(j).start()

    def second(v, carry):
        advance(v, 1)
        return carry

    lax.fori_loop(days - LAG1, days, second, 0)

    stages = (
        (0, 0, days, lambda i: advance(i, 2)),
        (LAG3, 0, days, reduce_last),
        (LAG4, 0, days, assemble),
        (LAG5, 0, 2 * HALF, add_halo),
        (LAG4 + 2 * HALF, 0, HALF + 1, close),
    )

    def run(begin, end):
        def body(v, carry):
            for lag, lo, hi, stage in stages:
                i = v - lag
                if end - lag <= lo or begin - lag >= hi:
                    continue
                if begin - lag >= lo and end - lag <= hi:
                    stage(i)
                else:
                    pl.when((i >= lo) & (i < hi))(functools.partial(stage, i))
            return carry

        lax.fori_loop(begin, end, body, 0)

    def near(side):
        at = pl.ds(last if side == 0 else 0, 8)
        return pltpu.make_async_remote_copy(
            src_ref=mrg_s.at[at],
            dst_ref=near_s.at[side],
            send_sem=near_send.at[side],
            recv_sem=near_recv.at[side],
            device_id=after if side == 0 else before,
            device_id_type=MESH,
        )

    run(0, 8)
    for j in range(1, nz):
        share_sums(j).wait()
    merged = own_s[...]
    for j in range(1, nz):
        merged = merged + got_s[j - 1]
    line = lax.broadcasted_iota(jnp.int32, (24, LANES), 0)
    lane = lax.broadcasted_iota(jnp.int32, (24, LANES), 1)
    number = jnp.where(line == lane, merged[days : days + 1, 0:LANES], 0.0)
    number = jnp.sum(number, axis=1, keepdims=True)
    mrg_s[:, 0:width] = merged
    mrg_s[:, width:] = jnp.broadcast_to(number, (24, LANES))
    for side in range(2):
        near(side).start()
    ext_s[HALF : HALF + days] = mrg_s[0:days]

    run(8, 16)
    for side in range(2):
        near(side).wait()
    ext_s[0:HALF] = near_s[0, 0:HALF]
    ext_s[HALF + days : 2 * HALF + days] = near_s[1, 0:HALF]
    win = ext_s[0:24]
    for k in range(1, SPAN):
        win = win + ext_s[k : k + 24]
    win_sum = win[:, 0:width]
    win_count = win[:, width:]
    mean_s[:, 0:LANES] = win_sum[:, 0:LANES] / win_count
    mean_s[:, LANES:] = win_sum[:, LANES:] / win_count
    inverse = 1.0 / (win_count - 1.0)
    own = mean_s[:, pl.ds(pl.multiple_of(LANES * (z // 2), LANES), LANES)]
    own = jnp.where(even, own, turned(own))
    for d in range(days):
        own_m[d] = own[d : d + 1, 0:share]
    mean_copy = pltpu.make_async_copy(own_m, mean_ref, m_sem)
    mean_copy.start()
    column = jnp.concatenate([own, jnp.zeros((LANES - 24, LANES), f32)], axis=0).T[:share]
    for d in range(days):
        inv_s[d] = jnp.broadcast_to(inverse[d : d + 1], (8, LANES))
        outer = column[:, d : d + 1] * win_sum[d : d + 1]
        acc[d + 2 * HALF] = acc[d + 2 * HALF] - outer

    run(16, days + LAG4)

    def rest(d, carry):
        close(d)
        return carry

    lax.fori_loop(HALF + 1, days, rest, 0)

    def drain(i, carry):
        for k in range(nz - 1):
            send(i, k).wait_send()
            give_to(i, k + 1).wait_send()
        return carry

    lax.fori_loop(0, days, drain, 0)

    def drain_halo(i, carry):
        halo(i).wait_send()
        return carry

    lax.fori_loop(0, 2 * HALF, drain_halo, 0)
    mean_copy.wait()

    def written(d, carry):
        put(d).wait()
        return carry

    lax.fori_loop(0, days, written, 0)


def hand_over(cov_ref, mean_ref, cov_out, mean_out, cov_sem, mean_sem):
    big = pltpu.make_async_copy(cov_ref, cov_out, cov_sem)
    small = pltpu.make_async_copy(mean_ref, mean_out, mean_sem)
    big.start()
    small.start()
    big.wait()
    small.wait()


def shards(samples, counts):
    days, groups, slots, width = samples.shape
    nz = lax.axis_size("year")
    share = width // nz
    rows = share + share // nz
    low = slots // 2 // 16 * 16
    f32 = jnp.float32
    dma = pltpu.SemaphoreType.DMA
    covariance, mean = pl.pallas_call(
        functools.partial(kernel, low),
        out_shape=(
            jax.ShapeDtypeStruct((days, share, width), f32),
            jax.ShapeDtypeStruct((days, 1, share), f32),
        ),
        in_specs=[pl.BlockSpec(memory_space=pltpu.HBM), pl.BlockSpec(memory_space=pltpu.HBM)],
        out_specs=(pl.BlockSpec(memory_space=pl.ANY), pl.BlockSpec(memory_space=pl.ANY)),
        scratch_shapes=[
            pltpu.SMEM((groups, days), jnp.int32),
            pltpu.VMEM((SLOTS, groups, slots, width), samples.dtype),
            pltpu.VMEM((days, nz, rows, LANES), f32),
            pltpu.VMEM((nz - 1, days, rows, LANES), f32),
            pltpu.VMEM((days, 48, LANES), f32),
            pltpu.VMEM((days, 56, LANES), f32),
            pltpu.VMEM((share, LANES), f32),
            pltpu.VMEM((days + 2 * HALF, share, width), f32),
            pltpu.VMEM((days + 4 * HALF, share, width), f32),
            pltpu.VMEM((24, width), f32),
            pltpu.VMEM((nz - 1, 24, width), f32),
            pltpu.VMEM((24, width + LANES), f32),
            pltpu.VMEM((2, 8, width + LANES), f32),
            pltpu.VMEM((40, width + LANES), f32),
            pltpu.VMEM((24, width), f32),
            pltpu.VMEM((days, 8, LANES), f32),
            pltpu.VMEM((days, 1, share), f32),
            dma,
            dma((SLOTS,)),
            dma((days,)),
            dma,
            dma((nz - 1, days)),
            dma((nz - 1, days)),
            dma((nz - 1, days)),
            dma((nz - 1, days)),
            dma((2 * HALF,)),
            dma((2 * HALF,)),
            dma((nz - 1,)),
            dma((nz - 1,)),
            dma((2,)),
            dma((2,)),
        ],
        compiler_params=pltpu.CompilerParams(
            collective_id=0, has_side_effects=True, vmem_limit_bytes=44 * 2**20
        ),
    )(jnp.swapaxes(counts, 1, 2)[0], samples)
    covariance, mean = pl.pallas_call(
        hand_over,
        out_shape=(
            jax.ShapeDtypeStruct((days, share, width), f32),
            jax.ShapeDtypeStruct((days, 1, share), f32),
        ),
        in_specs=[pl.BlockSpec(memory_space=pl.ANY), pl.BlockSpec(memory_space=pl.ANY)],
        out_specs=(pl.BlockSpec(memory_space=pl.ANY), pl.BlockSpec(memory_space=pl.ANY)),
        scratch_shapes=[dma, dma],
        compiler_params=pltpu.CompilerParams(vmem_limit_bytes=2**20),
    )(covariance, mean)
    return (covariance[None], jnp.swapaxes(mean, 0, 1))


def solution(mesh):
    placed = (P("day", "year", "region", None), P("region", "day", "year"))
    return jax.shard_map(
        shards,
        mesh=mesh,
        in_specs=placed,
        out_specs=(P("region", "day", "year", None), P("region", "day", "year")),
        check_vma=False,
    )
```

```python
import functools

import jax
import jax.numpy as jnp
from jax import lax
from jax.experimental import pallas as pl
from jax.experimental.pallas import tpu as pltpu
from jax.sharding import PartitionSpec as P

HALF = 7
SPAN = 2 * HALF + 1
SLOTS = 8
AHEAD = 7
LANES = 128
LAG1 = 8
LAG3 = 6
LAG4 = 12
LAG5 = 17
MESH = pl.DeviceIdType.MESH


def turned(x):
    return pltpu.roll(x, LANES // 2, 1)


def flipped(x):
    return jnp.concatenate([x, x], axis=0).T


def kernel(
    low,
    cnt_ref,
    x_ref,
    out_ref,
    mean_ref,
    cnt,
    xbuf,
    pack,
    hop,
    give,
    take,
    tile,
    ext,
    acc,
    own_s,
    got_s,
    mrg_s,
    near_s,
    ext_s,
    mean_s,
    inv_s,
    c_sem,
    x_sem,
    hop_send,
    hop_recv,
    give_send,
    give_recv,
    halo_send,
    halo_recv,
    sum_send,
    sum_recv,
    near_send,
    near_recv,
):
    days, groups, slots, width = x_ref.shape
    f32 = jnp.float32
    z = lax.axis_index("year")
    q = lax.axis_index("day")
    nz = lax.axis_size("year")
    nq = lax.axis_size("day")
    share = width // nz
    quarter = share // nz
    rows = share + quarter // 2
    low32 = share // 2
    last = days - HALF
    even = lax.rem(z, 2) == 0
    after = {"day": lax.rem(q + 1, nq)}
    before = {"day": lax.rem(q + nq - 1, nq)}

    def peer(j):
        return {"year": lax.rem(z + j, nz)}

    def left(n):
        return lax.broadcasted_iota(jnp.int32, (n, LANES), 1) < LANES // 2

    barrier = pltpu.get_barrier_semaphore()
    for j in range(1, nz):
        pl.semaphore_signal(barrier, inc=1, device_id=peer(j), device_id_type=MESH)
    pl.semaphore_signal(barrier, inc=1, device_id=after, device_id_type=MESH)
    pl.semaphore_signal(barrier, inc=1, device_id=before, device_id_type=MESH)

    def day_of(i):
        return lax.rem(i + last, days)

    def step_of(i):
        return 1 + (nz - 2) * lax.rem(i + q, 2)

    def fetch(i):
        slot = lax.rem(i, SLOTS)
        return pltpu.make_async_copy(x_ref.at[day_of(i)], xbuf.at[slot], x_sem.at[slot])

    counted = pltpu.make_async_copy(cnt_ref, cnt, c_sem)
    counted.start()
    fetch(0).start()
    fetch(1).start()
    own_s[...] = jnp.zeros_like(own_s)
    ext_s[...] = jnp.zeros_like(ext_s)

    def clear(e, carry):
        acc[e] = jnp.zeros((share, width), f32)
        return carry

    lax.fori_loop(0, days + 4 * HALF, clear, 0)
    counted.wait()

    def compute(i, opening=False):
        slot = lax.rem(i, SLOTS)
        t = day_of(i)
        fetch(i).wait()
        if opening:
            for j in range(2, AHEAD + 1):
                fetch(j).start()
        else:

            @pl.when(i + AHEAD < days)
            def _():
                fetch(i + AHEAD).start()

        total = jnp.zeros((width, width), f32)
        sums = jnp.zeros((8, width), f32)
        count = jnp.int32(0)
        for g in range(groups):
            c = cnt[g, t]
            count = count + c
            head = xbuf[slot, g, 0:low, :]
            tail = xbuf[slot, g, low:slots, :]
            at = low + lax.broadcasted_iota(jnp.int32, tail.shape, 0)
            tail = jnp.where(at < c, tail, jnp.zeros_like(tail))
            for part in (head, tail):
                total = total + lax.dot_general(
                    part, part, (((0,), (0,)), ((), ())), preferred_element_type=f32
                )
                sums = sums + jnp.sum(part.astype(f32).reshape(-1, 8, width), axis=0)
        half = left(share)

        def cell(r, h):
            return total[share * r : share * (r + 1), LANES * h : LANES * (h + 1)]

        lane_no = lax.broadcasted_iota(jnp.int32, (share, LANES), 1)
        wide = lane_no * 0 + step_of(i) == 1
        main = (
            jnp.where(half | wide, cell(0, 0), cell(0, 1)),
            jnp.where(half & wide, cell(1, 1), cell(1, 0)),
            jnp.where(half | wide, cell(2, 1), cell(2, 0)),
            jnp.where(half & wide, cell(3, 0), cell(3, 1)),
        )
        across = jnp.where(half, cell(0, 1), cell(1, 1))
        gap = lax.broadcasted_iota(jnp.int32, (low32, LANES), 1) // 32
        for b in range(4):
            spare = across[quarter * b + 8 : quarter * (b + 1)]
            start = (b % 2) * (LANES // 2)
            strips = [
                spare if (start - 32 * k) % LANES == 0 else pltpu.roll(spare, (start - 32 * k) % LANES, 1)
                for k in range(4)
            ]
            pack[i, b, 0:low32] = main[b][0:low32]
            pack[i, b, low32:share] = jnp.where(
                gap == 2 * (b % 2), jnp.concatenate(strips, axis=0), main[b][low32:]
            )
            pack[i, b, share:rows] = across[quarter * b : quarter * b + 8]
        line = lax.broadcasted_iota(jnp.int32, (24, width), 0)
        lane = lax.broadcasted_iota(jnp.int32, (24, width), 1)
        kept = jnp.where(line == t, jnp.sum(sums, axis=0, keepdims=True), own_s[...])
        number = jnp.full((24, width), count, jnp.int32).astype(f32)
        own_s[...] = jnp.where((line == days) & (lane == t), number, kept)

    def block(i, k):
        return lax.rem(z + (nz - step_of(i)) * (k + 1), nz)

    def send(i, k):
        return pltpu.make_async_remote_copy(
            src_ref=pack.at[i, block(i, 0)] if k == 0 else hop.at[k - 1, i],
            dst_ref=hop.at[k, i],
            send_sem=hop_send.at[k, i],
            recv_sem=hop_recv.at[k, i],
            device_id=peer(step_of(i)),
            device_id_type=MESH,
        )

    def advance(i, k):
        send(i, k - 1).wait_recv()
        hop[k - 1, i] = hop[k - 1, i] + pack[i, block(i, k)]
        send(i, k).start()

    def give_to(i, j):
        start, size, land = ((0, 40, 0), (40, 8, 48), (32, 8, 40))[j - 1]
        to = (step_of(i), 2, nz - step_of(i))[j - 1]
        return pltpu.make_async_remote_copy(
            src_ref=give.at[i, pl.ds(start, size)],
            dst_ref=take.at[i, pl.ds(land, size)],
            send_sem=give_send.at[j - 1, i],
            recv_sem=give_recv.at[j - 1, i],
            device_id=peer(to),
            device_id_type=MESH,
        )

    def reduce_last(i):
        send(i, 2).wait_recv()
        mine = hop[2, i] + pack[i, z]
        main = mine[0:share]
        both = flipped(main)
        turn = jnp.where(even, both[share:], both[:share])
        mirror = jnp.where(even, both[:share], both[share:])
        lane32 = lax.broadcasted_iota(jnp.int32, (share, LANES), 1) // 32
        deep = lax.broadcasted_iota(jnp.int32, (share, LANES), 0) >= low32
        hop[2, i, 0:share] = jnp.where(deep & (lane32 == 2 * lax.rem(z, 2)), mirror, main)
        strips = main[low32:]
        strips = jnp.where(even, strips, turned(strips))
        spare = strips[0:8]
        for k in range(1, 4):
            spare = jnp.where(lane32[0:8] == k, pltpu.roll(strips[8 * k : 8 * k + 8], 32 * k, 1), spare)
        edge = jnp.concatenate([mine[share:rows], spare], axis=0)
        edge_t = turned(edge)
        half8 = left(8)
        lefts = jnp.where(half8, edge[0:8], edge_t[8:16])
        rights = jnp.where(half8, edge_t[0:8], edge[8:16])
        give[i, 0:low32] = jnp.where(left(low32), turn[0:low32], turn[low32:])
        give[i, 32:40] = jnp.where(even, rights, lefts)
        give[i, 40:48] = jnp.where(even, lefts, rights)
        for j in range(1, nz):
            give_to(i, j).start()

    def halo(i):
        side = i // HALF
        return pltpu.make_async_remote_copy(
            src_ref=ext.at[day_of(i) + HALF],
            dst_ref=ext.at[i + days * side],
            send_sem=halo_send.at[i],
            recv_sem=halo_recv.at[i],
            device_id={"day": lax.rem(q + 1 + (nq - 2) * side, nq)},
            device_id_type=MESH,
        )

    def add_day(e):
        value = ext[e]

        def one(k, carry):
            acc[e + k] = acc[e + k] + value
            return carry

        lax.fori_loop(0, SPAN, one, 0)

    def assemble(i):
        for j in range(1, nz):
            give_to(i, j).wait_recv()
        pieces = (give[i, 40:48], take[i, 40:48], take[i, 48:56], take[i, 32:40])
        s = step_of(i)
        for j, piece in zip((0, s, 2, nz - s), pieces):
            at = quarter * lax.rem(z + j, nz)
            tile[pl.ds(pl.multiple_of(at, 8), 8)] = piece
            tile[pl.ds(pl.multiple_of(at + 8, 8), 8)] = turned(piece)
        flat = tile[...]
        straight = jnp.where(z == 0, flat, turned(flat))
        opposite = jnp.where(z < 2, straight, flipped(flat)[:share])
        near_p = take[i, 0:32]
        near_t = turned(near_p)
        beside = jnp.where(
            even,
            jnp.concatenate([near_t, near_p], axis=0),
            jnp.concatenate([near_p, near_t], axis=0),
        )
        lane = lax.broadcasted_iota(jnp.int32, (share, LANES), 1) // (LANES // 2)
        other = jnp.where(lane == lax.rem(z, 2), opposite, beside)
        own_main = 1 - z // 2
        next_main = 1 - lax.rem(z + s, nz) // 2
        use = jnp.where(lane == lax.rem(z, 2), own_main, next_main) == 1
        main = hop[2, i, 0:share]
        e = day_of(i) + HALF
        ext[e, :, 0:LANES] = jnp.where(use, main, other)
        ext[e, :, LANES:] = jnp.where(use, other, main)

        @pl.when(i < 2 * HALF)
        def _():
            halo(i).start()

        add_day(e)

    def add_halo(i):
        halo(i).wait_recv()
        add_day(i + days * (i // HALF))

    def close(d):
        scale = inv_s[d][0:1]
        out_ref[d, :, 0:LANES] = acc[d + 2 * HALF, :, 0:LANES] * scale
        out_ref[d, :, LANES:] = acc[d + 2 * HALF, :, LANES:] * scale

    compute(0, True)
    pl.semaphore_wait(barrier, nz + 1)
    send(0, 0).start()

    def first(v, carry):
        compute(v)
        send(v, 0).start()

        @pl.when(v >= LAG1)
        def _():
            advance(v - LAG1, 1)

        return carry

    lax.fori_loop(1, days, first, 0)

    def share_sums(j):
        return pltpu.make_async_remote_copy(
            src_ref=own_s,
            dst_ref=got_s.at[j - 1],
            send_sem=sum_send.at[j - 1],
            recv_sem=sum_recv.at[j - 1],
            device_id=peer(j),
            device_id_type=MESH,
        )

    for j in range(1, nz):
        share_sums(j).start()

    def second(v, carry):
        advance(v, 1)
        return carry

    lax.fori_loop(days - LAG1, days, second, 0)

    stages = (
        (0, 0, days, lambda i: advance(i, 2)),
        (LAG3, 0, days, reduce_last),
        (LAG4, 0, days, assemble),
        (LAG5, 0, 2 * HALF, add_halo),
        (LAG4 + 2 * HALF, 0, HALF + 1, close),
    )

    def run(begin, end):
        def body(v, carry):
            for lag, lo, hi, stage in stages:
                i = v - lag
                if end - lag <= lo or begin - lag >= hi:
                    continue
                if begin - lag >= lo and end - lag <= hi:
                    stage(i)
                else:
                    pl.when((i >= lo) & (i < hi))(functools.partial(stage, i))
            return carry

        lax.fori_loop(begin, end, body, 0)

    def near(side):
        at = pl.ds(last if side == 0 else 0, 8)
        return pltpu.make_async_remote_copy(
            src_ref=mrg_s.at[at],
            dst_ref=near_s.at[side],
            send_sem=near_send.at[side],
            recv_sem=near_recv.at[side],
            device_id=after if side == 0 else before,
            device_id_type=MESH,
        )

    run(0, 8)
    for j in range(1, nz):
        share_sums(j).wait()
    merged = own_s[...]
    for j in range(1, nz):
        merged = merged + got_s[j - 1]
    line = lax.broadcasted_iota(jnp.int32, (24, LANES), 0)
    lane = lax.broadcasted_iota(jnp.int32, (24, LANES), 1)
    number = jnp.where(line == lane, merged[days : days + 1, 0:LANES], 0.0)
    number = jnp.sum(number, axis=1, keepdims=True)
    mrg_s[:, 0:width] = merged
    mrg_s[:, width:] = jnp.broadcast_to(number, (24, LANES))
    for side in range(2):
        near(side).start()
    ext_s[HALF : HALF + days] = mrg_s[0:days]

    run(8, 16)
    for side in range(2):
        near(side).wait()
    ext_s[0:HALF] = near_s[0, 0:HALF]
    ext_s[HALF + days : 2 * HALF + days] = near_s[1, 0:HALF]
    win = ext_s[0:24]
    for k in range(1, SPAN):
        win = win + ext_s[k : k + 24]
    win_sum = win[:, 0:width]
    win_count = win[:, width:]
    mean_s[:, 0:LANES] = win_sum[:, 0:LANES] / win_count
    mean_s[:, LANES:] = win_sum[:, LANES:] / win_count
    inverse = 1.0 / (win_count - 1.0)
    own = mean_s[:, pl.ds(pl.multiple_of(LANES * (z // 2), LANES), LANES)]
    own = jnp.where(even, own, turned(own))
    for d in range(days):
        mean_ref[d] = own[d : d + 1, 0:share]
    column = jnp.concatenate([own, jnp.zeros((LANES - 24, LANES), f32)], axis=0).T[:share]
    for d in range(days):
        inv_s[d] = jnp.broadcast_to(inverse[d : d + 1], (8, LANES))
        outer = column[:, d : d + 1] * win_sum[d : d + 1]
        acc[d + 2 * HALF] = acc[d + 2 * HALF] - outer

    run(16, days + LAG4)

    def rest(d, carry):
        close(d)
        return carry

    lax.fori_loop(HALF + 1, days, rest, 0)

    def drain(i, carry):
        for k in range(nz - 1):
            send(i, k).wait_send()
            give_to(i, k + 1).wait_send()
        return carry

    lax.fori_loop(0, days, drain, 0)

    def drain_halo(i, carry):
        halo(i).wait_send()
        return carry

    lax.fori_loop(0, 2 * HALF, drain_halo, 0)


def hand_over(cov_ref, mean_ref, cov_out, mean_out, cov_sem, mean_sem):
    big = pltpu.make_async_copy(cov_ref, cov_out, cov_sem)
    small = pltpu.make_async_copy(mean_ref, mean_out, mean_sem)
    big.start()
    small.start()
    big.wait()
    small.wait()


def shards(samples, counts):
    days, groups, slots, width = samples.shape
    nz = lax.axis_size("year")
    share = width // nz
    rows = share + share // nz // 2
    low = slots // 2 // 16 * 16
    f32 = jnp.float32
    dma = pltpu.SemaphoreType.DMA
    covariance, mean = pl.pallas_call(
        functools.partial(kernel, low),
        out_shape=(
            jax.ShapeDtypeStruct((days, share, width), f32),
            jax.ShapeDtypeStruct((days, 1, share), f32),
        ),
        in_specs=[pl.BlockSpec(memory_space=pltpu.HBM), pl.BlockSpec(memory_space=pltpu.HBM)],
        out_specs=(pl.BlockSpec(memory_space=pltpu.VMEM), pl.BlockSpec(memory_space=pltpu.VMEM)),
        scratch_shapes=[
            pltpu.SMEM((groups, days), jnp.int32),
            pltpu.VMEM((SLOTS, groups, slots, width), samples.dtype),
            pltpu.VMEM((days, nz, rows, LANES), f32),
            pltpu.VMEM((nz - 1, days, rows, LANES), f32),
            pltpu.VMEM((days, 48, LANES), f32),
            pltpu.VMEM((days, 56, LANES), f32),
            pltpu.VMEM((share, LANES), f32),
            pltpu.VMEM((days + 2 * HALF, share, width), f32),
            pltpu.VMEM((days + 4 * HALF, share, width), f32),
            pltpu.VMEM((24, width), f32),
            pltpu.VMEM((nz - 1, 24, width), f32),
            pltpu.VMEM((24, width + LANES), f32),
            pltpu.VMEM((2, 8, width + LANES), f32),
            pltpu.VMEM((40, width + LANES), f32),
            pltpu.VMEM((24, width), f32),
            pltpu.VMEM((days, 8, LANES), f32),
            dma,
            dma((SLOTS,)),
            dma((nz - 1, days)),
            dma((nz - 1, days)),
            dma((nz - 1, days)),
            dma((nz - 1, days)),
            dma((2 * HALF,)),
            dma((2 * HALF,)),
            dma((nz - 1,)),
            dma((nz - 1,)),
            dma((2,)),
            dma((2,)),
        ],
        compiler_params=pltpu.CompilerParams(
            collective_id=0, has_side_effects=True, vmem_limit_bytes=44 * 2**20
        ),
    )(pltpu.with_memory_space_constraint(jnp.swapaxes(counts, 1, 2)[0], pltpu.HBM), samples)
    covariance, mean = pl.pallas_call(
        hand_over,
        out_shape=(
            jax.ShapeDtypeStruct((days, share, width), f32),
            jax.ShapeDtypeStruct((days, 1, share), f32),
        ),
        in_specs=[pl.BlockSpec(memory_space=pl.ANY), pl.BlockSpec(memory_space=pl.ANY)],
        out_specs=(pl.BlockSpec(memory_space=pl.ANY), pl.BlockSpec(memory_space=pl.ANY)),
        scratch_shapes=[dma, dma],
        compiler_params=pltpu.CompilerParams(vmem_limit_bytes=2**20),
    )(covariance, mean)
    return (covariance[None], jnp.swapaxes(mean, 0, 1))


def solution(mesh):
    placed = (P("day", "year", "region", None), P("region", "day", "year"))
    return jax.shard_map(
        shards,
        mesh=mesh,
        in_specs=placed,
        out_specs=(P("region", "day", "year", None), P("region", "day", "year")),
        check_vma=False,
    )
```

```python
import functools

import jax
import jax.numpy as jnp
from jax import lax
from jax.experimental import pallas as pl
from jax.experimental.pallas import tpu as pltpu
from jax.sharding import PartitionSpec as P

HALF = 7
SPAN = 2 * HALF + 1
SLOTS = 8
AHEAD = 7
LANES = 128
LAG1 = 8
LAG3 = 6
LAG4 = 12
LAG5 = 20
MESH = pl.DeviceIdType.MESH


def turned(x):
    return pltpu.roll(x, LANES // 2, 1)


def flipped(x):
    return jnp.concatenate([x, x], axis=0).T


def kernel(
    low,
    cnt_ref,
    x_ref,
    out_ref,
    mean_ref,
    cnt,
    xbuf,
    pack,
    hop,
    give,
    take,
    tile,
    ext,
    acc,
    own_s,
    got_s,
    mrg_s,
    near_s,
    ext_s,
    mean_s,
    inv_s,
    c_sem,
    x_sem,
    hop_send,
    hop_recv,
    give_send,
    give_recv,
    halo_send,
    halo_recv,
    sum_send,
    sum_recv,
    near_send,
    near_recv,
):
    days, groups, slots, width = x_ref.shape
    f32 = jnp.float32
    z = lax.axis_index("year")
    q = lax.axis_index("day")
    nz = lax.axis_size("year")
    nq = lax.axis_size("day")
    share = width // nz
    quarter = share // nz
    rows = share + quarter // 2
    low32 = share // 2
    last = days - HALF
    even = lax.rem(z, 2) == 0
    after = {"day": lax.rem(q + 1, nq)}
    before = {"day": lax.rem(q + nq - 1, nq)}

    def peer(j):
        return {"year": lax.rem(z + j, nz)}

    def left(n):
        return lax.broadcasted_iota(jnp.int32, (n, LANES), 1) < LANES // 2

    barrier = pltpu.get_barrier_semaphore()
    for j in range(1, nz):
        pl.semaphore_signal(barrier, inc=1, device_id=peer(j), device_id_type=MESH)
    pl.semaphore_signal(barrier, inc=1, device_id=after, device_id_type=MESH)
    pl.semaphore_signal(barrier, inc=1, device_id=before, device_id_type=MESH)

    def day_of(i):
        return lax.rem(i + last, days)

    def step_of(i):
        return 1 + (nz - 2) * lax.rem(i + q, 2)

    def fetch(i):
        slot = lax.rem(i, SLOTS)
        return pltpu.make_async_copy(x_ref.at[day_of(i)], xbuf.at[slot], x_sem.at[slot])

    counted = pltpu.make_async_copy(cnt_ref, cnt, c_sem)
    counted.start()
    fetch(0).start()
    fetch(1).start()
    own_s[...] = jnp.zeros_like(own_s)
    ext_s[...] = jnp.zeros_like(ext_s)

    def clear(e, carry):
        acc[e] = jnp.zeros((share, width), f32)
        return carry

    lax.fori_loop(0, days + 4 * HALF, clear, 0)
    counted.wait()

    def compute(i, opening=False):
        slot = lax.rem(i, SLOTS)
        t = day_of(i)
        fetch(i).wait()
        if opening:
            for j in range(2, AHEAD + 1):
                fetch(j).start()
        else:

            @pl.when(i + AHEAD < days)
            def _():
                fetch(i + AHEAD).start()

        total = jnp.zeros((width, width), f32)
        sums = jnp.zeros((8, width), f32)
        count = jnp.int32(0)
        for g in range(groups):
            c = cnt[g, t]
            count = count + c
            head = xbuf[slot, g, 0:low, :]
            tail = xbuf[slot, g, low:slots, :]
            at = low + lax.broadcasted_iota(jnp.int32, tail.shape, 0)
            tail = jnp.where(at < c, tail, jnp.zeros_like(tail))
            for part in (head, tail):
                total = total + lax.dot_general(
                    part, part, (((0,), (0,)), ((), ())), preferred_element_type=f32
                )
                sums = sums + jnp.sum(part.astype(f32).reshape(-1, 8, width), axis=0)
        half = left(share)

        def cell(r, h):
            return total[share * r : share * (r + 1), LANES * h : LANES * (h + 1)]

        lane_no = lax.broadcasted_iota(jnp.int32, (share, LANES), 1)
        wide = lane_no * 0 + step_of(i) == 1
        main = (
            jnp.where(half | wide, cell(0, 0), cell(0, 1)),
            jnp.where(half & wide, cell(1, 1), cell(1, 0)),
            jnp.where(half | wide, cell(2, 1), cell(2, 0)),
            jnp.where(half & wide, cell(3, 0), cell(3, 1)),
        )
        across = jnp.where(half, cell(0, 1), cell(1, 1))
        gap = lax.broadcasted_iota(jnp.int32, (low32, LANES), 1) // 32
        for b in range(4):
            spare = across[quarter * b + 8 : quarter * (b + 1)]
            start = (b % 2) * (LANES // 2)
            strips = [
                spare if (start - 32 * k) % LANES == 0 else pltpu.roll(spare, (start - 32 * k) % LANES, 1)
                for k in range(4)
            ]
            pack[i, b, 0:low32] = main[b][0:low32]
            pack[i, b, low32:share] = jnp.where(
                gap == 2 * (b % 2), jnp.concatenate(strips, axis=0), main[b][low32:]
            )
            pack[i, b, share:rows] = across[quarter * b : quarter * b + 8]
        line = lax.broadcasted_iota(jnp.int32, (24, width), 0)
        lane = lax.broadcasted_iota(jnp.int32, (24, width), 1)
        kept = jnp.where(line == t, jnp.sum(sums, axis=0, keepdims=True), own_s[...])
        number = jnp.full((24, width), count, jnp.int32).astype(f32)
        own_s[...] = jnp.where((line == days) & (lane == t), number, kept)

    def block(i, k):
        return lax.rem(z + (nz - step_of(i)) * (k + 1), nz)

    def send(i, k):
        return pltpu.make_async_remote_copy(
            src_ref=pack.at[i, block(i, 0)] if k == 0 else hop.at[k - 1, i],
            dst_ref=hop.at[k, i],
            send_sem=hop_send.at[k, i],
            recv_sem=hop_recv.at[k, i],
            device_id=peer(step_of(i)),
            device_id_type=MESH,
        )

    def advance(i, k):
        send(i, k - 1).wait_recv()
        hop[k - 1, i] = hop[k - 1, i] + pack[i, block(i, k)]
        send(i, k).start()

    def give_to(i, j):
        start, size, land = ((0, 40, 0), (40, 8, 48), (32, 8, 40))[j - 1]
        to = (step_of(i), 2, nz - step_of(i))[j - 1]
        return pltpu.make_async_remote_copy(
            src_ref=give.at[i, pl.ds(start, size)],
            dst_ref=take.at[i, pl.ds(land, size)],
            send_sem=give_send.at[j - 1, i],
            recv_sem=give_recv.at[j - 1, i],
            device_id=peer(to),
            device_id_type=MESH,
        )

    def reduce_last(i):
        send(i, 2).wait_recv()
        mine = hop[2, i] + pack[i, z]
        main = mine[0:share]
        both = flipped(main)
        turn = jnp.where(even, both[share:], both[:share])
        mirror = jnp.where(even, both[:share], both[share:])
        lane32 = lax.broadcasted_iota(jnp.int32, (share, LANES), 1) // 32
        deep = lax.broadcasted_iota(jnp.int32, (share, LANES), 0) >= low32
        hop[2, i, 0:share] = jnp.where(deep & (lane32 == 2 * lax.rem(z, 2)), mirror, main)
        strips = main[low32:]
        strips = jnp.where(even, strips, turned(strips))
        spare = strips[0:8]
        for k in range(1, 4):
            spare = jnp.where(lane32[0:8] == k, pltpu.roll(strips[8 * k : 8 * k + 8], 32 * k, 1), spare)
        edge = jnp.concatenate([mine[share:rows], spare], axis=0)
        edge_t = turned(edge)
        half8 = left(8)
        lefts = jnp.where(half8, edge[0:8], edge_t[8:16])
        rights = jnp.where(half8, edge_t[0:8], edge[8:16])
        give[i, 0:low32] = jnp.where(left(low32), turn[0:low32], turn[low32:])
        give[i, 32:40] = jnp.where(even, rights, lefts)
        give[i, 40:48] = jnp.where(even, lefts, rights)
        for j in range(1, nz):
            give_to(i, j).start()

    def halo(i):
        side = i // HALF
        return pltpu.make_async_remote_copy(
            src_ref=ext.at[day_of(i) + HALF],
            dst_ref=ext.at[i + days * side],
            send_sem=halo_send.at[i],
            recv_sem=halo_recv.at[i],
            device_id={"day": lax.rem(q + 1 + (nq - 2) * side, nq)},
            device_id_type=MESH,
        )

    def add_day(e):
        value = ext[e]

        def one(k, carry):
            acc[e + k] = acc[e + k] + value
            return carry

        lax.fori_loop(0, SPAN, one, 0, unroll=5)

    def assemble(i):
        for j in range(1, nz):
            give_to(i, j).wait_recv()
        pieces = (give[i, 40:48], take[i, 40:48], take[i, 48:56], take[i, 32:40])
        s = step_of(i)
        for j, piece in zip((0, s, 2, nz - s), pieces):
            at = quarter * lax.rem(z + j, nz)
            tile[pl.ds(pl.multiple_of(at, 8), 8)] = piece
            tile[pl.ds(pl.multiple_of(at + 8, 8), 8)] = turned(piece)
        flat = tile[...]
        straight = jnp.where(z == 0, flat, turned(flat))
        opposite = jnp.where(z < 2, straight, flipped(flat)[:share])
        near_p = take[i, 0:32]
        near_t = turned(near_p)
        beside = jnp.where(
            even,
            jnp.concatenate([near_t, near_p], axis=0),
            jnp.concatenate([near_p, near_t], axis=0),
        )
        lane = lax.broadcasted_iota(jnp.int32, (share, LANES), 1) // (LANES // 2)
        other = jnp.where(lane == lax.rem(z, 2), opposite, beside)
        own_main = 1 - z // 2
        next_main = 1 - lax.rem(z + s, nz) // 2
        use = jnp.where(lane == lax.rem(z, 2), own_main, next_main) == 1
        main = hop[2, i, 0:share]
        e = day_of(i) + HALF
        ext[e, :, 0:LANES] = jnp.where(use, main, other)
        ext[e, :, LANES:] = jnp.where(use, other, main)

        @pl.when(i < 2 * HALF)
        def _():
            halo(i).start()

        add_day(e)

    def add_halo(i):
        halo(i).wait_recv()
        add_day(i + days * (i // HALF))

    def close(d):
        scale = inv_s[d][0:1]
        out_ref[d, :, 0:LANES] = acc[d + 2 * HALF, :, 0:LANES] * scale
        out_ref[d, :, LANES:] = acc[d + 2 * HALF, :, LANES:] * scale

    compute(0, True)
    pl.semaphore_wait(barrier, nz + 1)
    send(0, 0).start()

    def first(v, carry):
        compute(v)
        send(v, 0).start()

        @pl.when(v >= LAG1)
        def _():
            advance(v - LAG1, 1)

        return carry

    lax.fori_loop(1, days, first, 0)

    def share_sums(j):
        return pltpu.make_async_remote_copy(
            src_ref=own_s,
            dst_ref=got_s.at[j - 1],
            send_sem=sum_send.at[j - 1],
            recv_sem=sum_recv.at[j - 1],
            device_id=peer(j),
            device_id_type=MESH,
        )

    for j in range(1, nz):
        share_sums(j).start()

    def second(v, carry):
        advance(v, 1)
        return carry

    lax.fori_loop(days - LAG1, days, second, 0)

    stages = (
        (0, 0, days, lambda i: advance(i, 2)),
        (LAG3, 0, days, reduce_last),
        (LAG4, 0, days, assemble),
        (LAG5, 0, 2 * HALF, add_halo),
        (LAG4 + 2 * HALF, 0, HALF + 1, close),
    )

    def run(begin, end):
        def body(v, carry):
            for lag, lo, hi, stage in stages:
                i = v - lag
                if end - lag <= lo or begin - lag >= hi:
                    continue
                if begin - lag >= lo and end - lag <= hi:
                    stage(i)
                else:
                    pl.when((i >= lo) & (i < hi))(functools.partial(stage, i))
            return carry

        lax.fori_loop(begin, end, body, 0)

    def near(side):
        at = pl.ds(last if side == 0 else 0, 8)
        return pltpu.make_async_remote_copy(
            src_ref=mrg_s.at[at],
            dst_ref=near_s.at[side],
            send_sem=near_send.at[side],
            recv_sem=near_recv.at[side],
            device_id=after if side == 0 else before,
            device_id_type=MESH,
        )

    run(0, 8)
    for j in range(1, nz):
        share_sums(j).wait()
    merged = own_s[...]
    for j in range(1, nz):
        merged = merged + got_s[j - 1]
    line = lax.broadcasted_iota(jnp.int32, (24, LANES), 0)
    lane = lax.broadcasted_iota(jnp.int32, (24, LANES), 1)
    number = jnp.where(line == lane, merged[days : days + 1, 0:LANES], 0.0)
    number = jnp.sum(number, axis=1, keepdims=True)
    mrg_s[:, 0:width] = merged
    mrg_s[:, width:] = jnp.broadcast_to(number, (24, LANES))
    for side in range(2):
        near(side).start()
    ext_s[HALF : HALF + days] = mrg_s[0:days]

    run(8, 16)
    for side in range(2):
        near(side).wait()
    ext_s[0:HALF] = near_s[0, 0:HALF]
    ext_s[HALF + days : 2 * HALF + days] = near_s[1, 0:HALF]
    win = ext_s[0:24]
    for k in range(1, SPAN):
        win = win + ext_s[k : k + 24]
    win_sum = win[:, 0:width]
    win_count = win[:, width:]
    mean_s[:, 0:LANES] = win_sum[:, 0:LANES] / win_count
    mean_s[:, LANES:] = win_sum[:, LANES:] / win_count
    inverse = 1.0 / (win_count - 1.0)
    own = mean_s[:, pl.ds(pl.multiple_of(LANES * (z // 2), LANES), LANES)]
    own = jnp.where(even, own, turned(own))
    for d in range(days):
        mean_ref[d] = own[d : d + 1, 0:share]
    column = jnp.concatenate([own, jnp.zeros((LANES - 24, LANES), f32)], axis=0).T[:share]
    for d in range(days):
        inv_s[d] = jnp.broadcast_to(inverse[d : d + 1], (8, LANES))
        outer = column[:, d : d + 1] * win_sum[d : d + 1]
        acc[d + 2 * HALF] = acc[d + 2 * HALF] - outer

    run(16, days + LAG4)

    def rest(d, carry):
        close(d)
        return carry

    lax.fori_loop(HALF + 1, days, rest, 0)

    def drain(i, carry):
        for k in range(nz - 1):
            send(i, k).wait_send()
            give_to(i, k + 1).wait_send()
        return carry

    lax.fori_loop(0, days, drain, 0)

    def drain_halo(i, carry):
        halo(i).wait_send()
        return carry

    lax.fori_loop(0, 2 * HALF, drain_halo, 0)


def hand_over(cov_ref, mean_ref, cov_out, mean_out, cov_sem, mean_sem):
    big = pltpu.make_async_copy(cov_ref, cov_out, cov_sem)
    small = pltpu.make_async_copy(mean_ref, mean_out, mean_sem)
    big.start()
    small.start()
    big.wait()
    small.wait()


def shards(samples, counts):
    days, groups, slots, width = samples.shape
    nz = lax.axis_size("year")
    share = width // nz
    rows = share + share // nz // 2
    low = slots // 2 // 16 * 16
    f32 = jnp.float32
    dma = pltpu.SemaphoreType.DMA
    covariance, mean = pl.pallas_call(
        functools.partial(kernel, low),
        out_shape=(
            jax.ShapeDtypeStruct((days, share, width), f32),
            jax.ShapeDtypeStruct((days, 1, share), f32),
        ),
        in_specs=[pl.BlockSpec(memory_space=pltpu.HBM), pl.BlockSpec(memory_space=pltpu.HBM)],
        out_specs=(pl.BlockSpec(memory_space=pltpu.VMEM), pl.BlockSpec(memory_space=pltpu.VMEM)),
        scratch_shapes=[
            pltpu.SMEM((groups, days), jnp.int32),
            pltpu.VMEM((SLOTS, groups, slots, width), samples.dtype),
            pltpu.VMEM((days, nz, rows, LANES), f32),
            pltpu.VMEM((nz - 1, days, rows, LANES), f32),
            pltpu.VMEM((days, 48, LANES), f32),
            pltpu.VMEM((days, 56, LANES), f32),
            pltpu.VMEM((share, LANES), f32),
            pltpu.VMEM((days + 2 * HALF, share, width), f32),
            pltpu.VMEM((days + 4 * HALF, share, width), f32),
            pltpu.VMEM((24, width), f32),
            pltpu.VMEM((nz - 1, 24, width), f32),
            pltpu.VMEM((24, width + LANES), f32),
            pltpu.VMEM((2, 8, width + LANES), f32),
            pltpu.VMEM((40, width + LANES), f32),
            pltpu.VMEM((24, width), f32),
            pltpu.VMEM((days, 8, LANES), f32),
            dma,
            dma((SLOTS,)),
            dma((nz - 1, days)),
            dma((nz - 1, days)),
            dma((nz - 1, days)),
            dma((nz - 1, days)),
            dma((2 * HALF,)),
            dma((2 * HALF,)),
            dma((nz - 1,)),
            dma((nz - 1,)),
            dma((2,)),
            dma((2,)),
        ],
        compiler_params=pltpu.CompilerParams(
            collective_id=0, has_side_effects=True, vmem_limit_bytes=44 * 2**20
        ),
    )(pltpu.with_memory_space_constraint(jnp.swapaxes(counts, 1, 2)[0], pltpu.HBM), samples)
    covariance, mean = pl.pallas_call(
        hand_over,
        out_shape=(
            jax.ShapeDtypeStruct((days, share, width), f32),
            jax.ShapeDtypeStruct((days, 1, share), f32),
        ),
        in_specs=[pl.BlockSpec(memory_space=pl.ANY), pl.BlockSpec(memory_space=pl.ANY)],
        out_specs=(pl.BlockSpec(memory_space=pl.ANY), pl.BlockSpec(memory_space=pl.ANY)),
        scratch_shapes=[dma, dma],
        compiler_params=pltpu.CompilerParams(vmem_limit_bytes=2**20),
    )(covariance, mean)
    return (covariance[None], jnp.swapaxes(mean, 0, 1))


def solution(mesh):
    placed = (P("day", "year", "region", None), P("region", "day", "year"))
    return jax.shard_map(
        shards,
        mesh=mesh,
        in_specs=placed,
        out_specs=(P("region", "day", "year", None), P("region", "day", "year")),
        check_vma=False,
    )
```
